32 devices in a mesh: ctx: 8 (over z, x), chan: 4 (over y, core).
Axes of the slice: x: 2, y: 2, z: 4, core: 2. Of those that a mesh axis runs over, the one named last changes fastest.
Arguments:
- query_in: bfloat16 [4096, 1024], P('chan', 'ctx'), may hold values from -6 to 6
- key_in: bfloat16 [4096, 1024], P('chan', 'ctx'), may hold values from -6 to 6
- value_in: bfloat16 [4096, 1024], P('chan', 'ctx'), may hold values from -6 to 6
- short_kernel: float32 [3, 3, 4096], P(None, None, 'chan'), may hold values from -3.5 to 3.5
- filter_in: float32 [64, 64], replicated, may hold values from -0.75 to 0.75
- filter_out: float32 [64, 4096], P(None, 'chan'), may hold values from -0.75 to 0.75
- filter_decay: float32 [4096], P('chan'), may hold values from 0.5 to 40
- skip_gain: float32 [4096], P('chan'), may hold values from -3 to 3
- grad_out: bfloat16 [4096, 1024], P('chan', 'ctx'), may hold values from -6 to 6
Outputs:
- output: bfloat16 [4096, 1024], P('chan', 'ctx')
- grad_query: bfloat16 [4096, 1024], P('chan', 'ctx')
- grad_key: bfloat16 [4096, 1024], P('chan', 'ctx')
- grad_value: bfloat16 [4096, 1024], P('chan', 'ctx')
- grad_short: float32 [3, 3, 4096], P(None, None, 'chan')
- grad_filter_in: float32 [64, 64], replicated
- grad_filter_out: float32 [64, 4096], P(None, 'chan')
- grad_decay: float32 [4096], P('chan')
- grad_skip: float32 [4096], P('chan')
The draws below stay inside these ranges and needn't reach their ends.
All inputs are finite; a program needn't handle non-finite values.
Results may differ from the reference program's by a relative error of at most 0.0006.
Values may be sent and summed in bfloat16 or wider, within the bound.
No kernel may reach another device: no remote copies, remote signals or barrier semaphores. Data moves between devices by JAX's collectives and lax.ppermute only.
A program may use at most 128 MiB of HBM per device.

```python
import math
import jax
import jax.numpy as jnp
from jax import lax

C = 4096
FEAT = 64
ORDER = 64
TOKENS = 1024


def block_levels(key, shape, shards, smallest, high):
    def one(dim, shards_of):
        heights = jax.random.uniform(jax.random.fold_in(jax.random.fold_in(key, 6), dim), (shards_of,), jnp.float32, smallest / len(shards), high / len(shards))
        return jnp.repeat(jnp.exp(heights), shape[dim] // shards_of).reshape((-1,) + (1,) * (len(shape) - dim - 1))

    gain = one(*shards[0])
    for cut in shards[1:]:
        gain = gain * one(*cut)
    return gain


def scatter_about(rng, dims, spread, most, shards=(), kind=jnp.bfloat16):
    values = spread * jax.random.normal(rng, dims, jnp.float32)
    if shards:
        values = values * block_levels(rng, dims, shards, -0.22, 0.18)
    return jnp.clip(values, -most, most).astype(kind)


def setup_inputs(seed: int = 0) -> dict:
    arg_keys = jax.random.split(jax.random.key(seed), 10)
    query_in = scatter_about(arg_keys[0], (C, TOKENS), 1.0, 6.0, ((0, 4), (1, 8)))
    key_in = scatter_about(arg_keys[1], (C, TOKENS), 1.0, 6.0, ((0, 4), (1, 8)))
    value_in = scatter_about(arg_keys[2], (C, TOKENS), 1.0, 6.0, ((0, 4), (1, 8)))
    short_kernel = scatter_about(arg_keys[3], (3, 3, C), 3 ** -0.5, 3.5, ((2, 4),), jnp.float32)
    filter_in = scatter_about(arg_keys[4], (FEAT, ORDER), FEAT ** -0.5, 0.75, (), jnp.float32)
    filter_out = scatter_about(arg_keys[5], (ORDER, C), ORDER ** -0.5, 0.75, ((1, 4),), jnp.float32)
    filter_decay = jnp.clip(jnp.exp(math.log(40.0) - 4.3820266 * jax.random.uniform(arg_keys[6], (C,), jnp.float32) ** block_levels(arg_keys[6], (C,), ((0, 4),), -0.2, 0.2)), 0.5, 40.0)
    skip_gain = scatter_about(arg_keys[7], (C,), 1.0, 3.0, ((0, 4),), jnp.float32)
    grad_out = scatter_about(arg_keys[8], (C, TOKENS), 1.0, 6.0, ((0, 4), (1, 8)))
    return {"query_in": query_in, "key_in": key_in, "value_in": value_in, "short_kernel": short_kernel, "filter_in": filter_in, "filter_out": filter_out, "filter_decay": filter_decay, "skip_gain": skip_gain, "grad_out": grad_out}


PRECISE = lax.Precision.HIGHEST


def position_features(position, sequence, feature_rows):
    bands = jnp.arange(feature_rows // 2, dtype=jnp.int32)
    factor = 4 * (bands + 1) * (bands + 1)
    phase = (position[None, :] * factor[:, None]) % sequence
    angles = (2.0 * math.pi / sequence) * phase.astype(jnp.float32)
    return jnp.concatenate([jnp.cos(angles), jnp.sin(angles)], axis=0)


def short_filter(values, kernel):
    padded = jnp.pad(values, ((0, 0), (2, 0)))
    return kernel[0][:, None] * values + kernel[1][:, None] * padded[:, 1:-1] + kernel[2][:, None] * padded[:, :-2]


def short_adjoint(grads, kernel):
    padded = jnp.pad(grads, ((0, 0), (0, 2)))
    return kernel[0][:, None] * grads + kernel[1][:, None] * padded[:, 1:-1] + kernel[2][:, None] * padded[:, 2:]


def kernel_terms(grads, values):
    padded = jnp.pad(values, ((0, 0), (2, 0)))
    return jnp.stack([jnp.sum(grads * values, axis=1), jnp.sum(grads * padded[:, 1:-1], axis=1), jnp.sum(grads * padded[:, :-2], axis=1)])


def causal_conv(first, second):
    sequence = first.shape[1]
    padded = 2 * sequence
    product = jnp.fft.rfft(first, n=padded, axis=1) * jnp.fft.rfft(second, n=padded, axis=1)
    return jnp.fft.irfft(product, n=padded, axis=1)[:, :sequence].astype(jnp.float32)


def correlate(first, second):
    sequence = first.shape[1]
    padded = 2 * sequence
    product = jnp.fft.rfft(first, n=padded, axis=1) * jnp.conj(jnp.fft.rfft(second, n=padded, axis=1))
    return jnp.fft.irfft(product, n=padded, axis=1)[:, :sequence].astype(jnp.float32)


def reference(query_in, key_in, value_in, short_kernel, filter_in, filter_out, filter_decay, skip_gain, grad_out):
    sequence = query_in.shape[1]
    position = jnp.arange(sequence, dtype=jnp.int32)
    fraction = position.astype(jnp.float32) / sequence
    scale = sequence ** -0.5
    query_f = query_in.astype(jnp.float32)
    key_f = key_in.astype(jnp.float32)
    value_f = value_in.astype(jnp.float32)
    query_short = short_filter(query_f, short_kernel[0])
    key_short = short_filter(key_f, short_kernel[1])
    value_short = short_filter(value_f, short_kernel[2])
    gate = key_short * value_short
    basis = position_features(position, sequence, filter_in.shape[0])
    preact = jnp.dot(filter_in.T, basis, precision=PRECISE)
    hidden = jnp.sin(preact)
    window = jnp.exp(-filter_decay[:, None] * fraction[None, :])
    taps = window * jnp.dot(filter_out.T, hidden, precision=PRECISE) * scale
    mixed = causal_conv(taps, gate) + skip_gain[:, None] * gate
    output = (query_short * mixed).astype(jnp.bfloat16)
    upstream = grad_out.astype(jnp.float32)
    grad_mixed = upstream * query_short
    grad_query_short = upstream * mixed
    grad_gate = correlate(grad_mixed, taps) + skip_gain[:, None] * grad_mixed
    grad_taps = correlate(grad_mixed, gate)
    grad_key_short = grad_gate * value_short
    grad_value_short = grad_gate * key_short
    grad_query = short_adjoint(grad_query_short, short_kernel[0]).astype(jnp.bfloat16)
    grad_key = short_adjoint(grad_key_short, short_kernel[1]).astype(jnp.bfloat16)
    grad_value = short_adjoint(grad_value_short, short_kernel[2]).astype(jnp.bfloat16)
    grad_short = jnp.stack([kernel_terms(grad_query_short, query_f), kernel_terms(grad_key_short, key_f), kernel_terms(grad_value_short, value_f)]) * scale
    weighted = grad_taps * window * scale
    grad_filter_out = jnp.dot(hidden, weighted.T, precision=PRECISE) * scale
    grad_hidden = jnp.dot(filter_out, weighted, precision=PRECISE)
    grad_filter_in = jnp.dot(basis, (grad_hidden * jnp.cos(preact)).T, precision=PRECISE) * scale
    grad_decay = jnp.sum(grad_taps * taps * (-fraction[None, :]), axis=1) * scale
    grad_skip = jnp.sum(grad_mixed * gate, axis=1) * scale
    return (output, grad_query, grad_key, grad_value, grad_short, grad_filter_in, grad_filter_out, grad_decay, grad_skip)
```

```python
import math

import jax
import jax.numpy as jnp
import numpy as np
from jax import lax
from jax.experimental import pallas as pl
from jax.experimental.pallas import tpu as pltpu
from jax.sharding import PartitionSpec as P

PRECISE = lax.Precision.HIGHEST


def shifted(value, axis, by):
    peers = lax.axis_size(axis)
    pairs = [(i, i + by) for i in range(peers) if 0 <= i + by < peers]
    return lax.ppermute(value, axis, pairs)


def position_features(position, sequence, feature_rows):
    bands = jnp.arange(feature_rows // 2, dtype=jnp.int32)
    factor = 4 * (bands + 1) * (bands + 1)
    phase = position[None, :] * factor[:, None] % sequence
    angles = 2.0 * math.pi / sequence * phase.astype(jnp.float32)
    return jnp.concatenate([jnp.cos(angles), jnp.sin(angles)], axis=0)


def angle_tables(left_index, right_index, modulus):
    phase = left_index[:, None] * right_index[None, :] % modulus
    angles = 2.0 * math.pi / modulus * phase.astype(jnp.float32)
    return (jnp.cos(angles), jnp.sin(angles))


def contract(form, left, right):
    return jnp.einsum(form, left, right, precision=PRECISE)


def times_forward(real_part, imag_part, cosine, sine):
    return (real_part * cosine + imag_part * sine, imag_part * cosine - real_part * sine)


def times_inverse(real_part, imag_part, cosine, sine):
    return (real_part * cosine - imag_part * sine, imag_part * cosine + real_part * sine)


def complex_times(first_real, first_imag, second_real, second_imag):
    return (
        first_real * second_real - first_imag * second_imag,
        first_real * second_imag + first_imag * second_real,
    )


def local_forward(real_part, imag_part):
    length = real_part.shape[-1]
    inner = 64
    outer = length // inner
    leading = real_part.shape[:-1]
    real_part = real_part.reshape(leading + (outer, inner))
    imag_part = imag_part.reshape(leading + (outer, inner))
    outer_index = jnp.arange(outer, dtype=jnp.int32)
    inner_index = jnp.arange(inner, dtype=jnp.int32)
    cos_outer, sin_outer = angle_tables(outer_index, outer_index, outer)
    first_real = contract("cb,...ba->...ca", cos_outer, real_part) + contract(
        "cb,...ba->...ca", sin_outer, imag_part
    )
    first_imag = contract("cb,...ba->...ca", cos_outer, imag_part) - contract(
        "cb,...ba->...ca", sin_outer, real_part
    )
    cos_middle, sin_middle = angle_tables(outer_index, inner_index, length)
    first_real, first_imag = times_forward(first_real, first_imag, cos_middle, sin_middle)
    cos_inner, sin_inner = angle_tables(inner_index, inner_index, inner)
    final_real = contract("...ca,da->...cd", first_real, cos_inner) + contract(
        "...ca,da->...cd", first_imag, sin_inner
    )
    final_imag = contract("...ca,da->...cd", first_imag, cos_inner) - contract(
        "...ca,da->...cd", first_real, sin_inner
    )
    return (final_real, final_imag)


def local_inverse(real_part, imag_part):
    outer = real_part.shape[-2]
    inner = real_part.shape[-1]
    length = outer * inner
    leading = real_part.shape[:-2]
    outer_index = jnp.arange(outer, dtype=jnp.int32)
    inner_index = jnp.arange(inner, dtype=jnp.int32)
    cos_inner, sin_inner = angle_tables(inner_index, inner_index, inner)
    first_real = contract("...cd,ad->...ca", real_part, cos_inner) - contract(
        "...cd,ad->...ca", imag_part, sin_inner
    )
    first_imag = contract("...cd,ad->...ca", imag_part, cos_inner) + contract(
        "...cd,ad->...ca", real_part, sin_inner
    )
    cos_middle, sin_middle = angle_tables(outer_index, inner_index, length)
    first_real, first_imag = times_inverse(first_real, first_imag, cos_middle, sin_middle)
    cos_outer, sin_outer = angle_tables(outer_index, outer_index, outer)
    final_real = contract("bc,...ca->...ba", cos_outer, first_real) - contract(
        "bc,...ca->...ba", sin_outer, first_imag
    )
    final_imag = contract("bc,...ca->...ba", cos_outer, first_imag) + contract(
        "bc,...ca->...ba", sin_outer, first_real
    )
    return (final_real.reshape(leading + (length,)), final_imag.reshape(leading + (length,)))


def held_frequencies(device):
    return 2 * device + jnp.arange(2, dtype=jnp.int32)


def forward_spectrum(signals):
    shards = lax.axis_size("ctx")
    device = lax.axis_index("ctx")
    signal_count, channels, length = signals.shape
    padded = 2 * shards * length
    columns = lax.all_to_all(
        signals.reshape((1, signal_count, channels, length)),
        "ctx",
        split_axis=3,
        concat_axis=0,
        tiled=True,
    )
    shard_index = jnp.arange(shards, dtype=jnp.int32)
    freq_index = jnp.arange(2 * shards, dtype=jnp.int32)
    cos_table, sin_table = angle_tables(freq_index, shard_index, 2 * shards)
    rows_real = contract("qp,pmgb->qmgb", cos_table, columns)
    rows_imag = -contract("qp,pmgb->qmgb", sin_table, columns)
    arrived = lax.all_to_all(
        jnp.stack([rows_real, rows_imag]), "ctx", split_axis=1, concat_axis=4, tiled=True
    )
    spec_real = arrived[0]
    spec_imag = arrived[1]
    freqs = held_frequencies(device)
    cosine, sine = angle_tables(freqs, jnp.arange(length, dtype=jnp.int32), padded)
    spec_real, spec_imag = times_forward(
        spec_real, spec_imag, cosine[:, None, None, :], sine[:, None, None, :]
    )
    return local_forward(spec_real, spec_imag)


def inverse_columns(spec_real, spec_imag):
    shards = lax.axis_size("ctx")
    device = lax.axis_index("ctx")
    real_part, imag_part = local_inverse(spec_real, spec_imag)
    length = real_part.shape[-1]
    padded = 2 * shards * length
    freqs = held_frequencies(device)
    cosine, sine = angle_tables(freqs, jnp.arange(length, dtype=jnp.int32), padded)
    real_part, imag_part = times_inverse(
        real_part, imag_part, cosine[:, None, None, :], sine[:, None, None, :]
    )
    shard_index = jnp.arange(shards, dtype=jnp.int32)
    arrived = lax.all_to_all(
        jnp.stack([real_part, imag_part]), "ctx", split_axis=4, concat_axis=1, tiled=True
    )
    cos_table, sin_table = angle_tables(
        shard_index, jnp.arange(2 * shards, dtype=jnp.int32), 2 * shards
    )
    columns = contract("pq,qmgb->pmgb", cos_table, arrived[0]) - contract(
        "pq,qmgb->pmgb", sin_table, arrived[1]
    )
    return columns * (1.0 / padded)


def to_tokens(columns):
    arrived = lax.all_to_all(columns, "ctx", split_axis=0, concat_axis=3, tiled=True)
    return arrived[0]


def spread_body(
    query_in,
    key_in,
    value_in,
    short_kernel,
    filter_in,
    filter_out,
    filter_decay,
    skip_gain,
    grad_out,
):
    shards = lax.axis_size("ctx")
    device = lax.axis_index("ctx")
    length = query_in.shape[1]
    sequence = shards * length
    scale = sequence ** (-0.5)
    inputs = jnp.stack([query_in, key_in, value_in])
    rim = shifted(inputs[:, :, -2:], "ctx", 1)
    values = inputs.astype(jnp.float32)
    rim_values = rim.astype(jnp.float32)
    before_one = jnp.concatenate([rim_values[..., 1:], values[..., :-1]], axis=-1)
    before_two = jnp.concatenate([rim_values, values[..., :-2]], axis=-1)
    kernel = short_kernel[:, :, :, None]
    shorted = kernel[:, 0] * values + kernel[:, 1] * before_one + kernel[:, 2] * before_two
    query_short = shorted[0]
    key_short = shorted[1]
    value_short = shorted[2]
    gate = key_short * value_short
    position = device * length + jnp.arange(length, dtype=jnp.int32)
    fraction = position.astype(jnp.float32) / sequence
    basis = position_features(position, sequence, filter_in.shape[0])
    preact = jnp.dot(filter_in.T, basis, precision=PRECISE)
    hidden = jnp.sin(preact)
    window = jnp.exp(-filter_decay[:, None] * fraction[None, :])
    taps = window * jnp.dot(filter_out.T, hidden, precision=PRECISE) * scale
    spec_real, spec_imag = forward_spectrum(jnp.stack([gate, taps]))
    gate_real, gate_imag = (spec_real[:, 0], spec_imag[:, 0])
    taps_real, taps_imag = (spec_real[:, 1], spec_imag[:, 1])
    prod_real, prod_imag = complex_times(gate_real, gate_imag, taps_real, taps_imag)
    conv = to_tokens(inverse_columns(prod_real[:, None], prod_imag[:, None]))[0]
    mixed = conv + skip_gain[:, None] * gate
    output = (query_short * mixed).astype(jnp.bfloat16)
    upstream = grad_out.astype(jnp.float32)
    grad_mixed = upstream * query_short
    grad_query_short = upstream * mixed
    upper_real, upper_imag = forward_spectrum(grad_mixed[None])
    upper_real = upper_real[:, 0]
    upper_imag = upper_imag[:, 0]
    along_real, along_imag = complex_times(taps_real, -taps_imag, upper_real, upper_imag)
    cross_real, cross_imag = complex_times(gate_real, -gate_imag, upper_real, upper_imag)
    backward = to_tokens(
        inverse_columns(
            jnp.stack([along_real, cross_real], axis=1), jnp.stack([along_imag, cross_imag], axis=1)
        )
    )
    grad_gate = backward[0] + skip_gain[:, None] * grad_mixed
    grad_taps = backward[1]
    grads = jnp.stack([grad_query_short, grad_gate * value_short, grad_gate * key_short])
    after = shifted(grads[..., :2], "ctx", -1)
    next_one = jnp.concatenate([grads[..., 1:], after[..., :1]], axis=-1)
    next_two = jnp.concatenate([grads[..., 2:], after], axis=-1)
    grad_inputs = (kernel[:, 0] * grads + kernel[:, 1] * next_one + kernel[:, 2] * next_two).astype(
        jnp.bfloat16
    )
    short_terms = jnp.stack(
        [
            jnp.sum(grads * values, axis=-1),
            jnp.sum(grads * before_one, axis=-1),
            jnp.sum(grads * before_two, axis=-1),
        ],
        axis=1,
    )
    weighted = grad_taps * window * scale
    out_terms = jnp.dot(hidden, weighted.T, precision=PRECISE)
    grad_hidden = jnp.dot(filter_out, weighted, precision=PRECISE)
    in_terms = jnp.dot(basis, (grad_hidden * jnp.cos(preact)).T, precision=PRECISE)
    decay_terms = jnp.sum(grad_taps * taps * -fraction[None, :], axis=1)
    skip_terms = jnp.sum(grad_mixed * gate, axis=1)
    short_sum, out_sum, decay_sum, skip_sum = lax.psum(
        (short_terms, out_terms, decay_terms, skip_terms), "ctx"
    )
    in_sum = lax.psum(in_terms, ("ctx", "chan"))
    return (
        output,
        grad_inputs[0],
        grad_inputs[1],
        grad_inputs[2],
        short_sum * scale,
        in_sum * scale,
        out_sum * scale,
        decay_sum * scale,
        skip_sum * scale,
    )


RADIX = 8
LANES = 128
ROOT_HALF = math.sqrt(0.5)
F32 = jnp.float32
BF16 = jnp.bfloat16


def split(value):
    high = value.astype(BF16)
    return high, (value - high.astype(F32)).astype(BF16)


def host_split(table):
    high = table.astype(BF16)
    low = (table - high.astype(np.float64)).astype(BF16)
    return high, low


def host_tables(sequence, feature_rows, length):
    outer = sequence // RADIX
    token = RADIX * np.arange(outer)[None, :] + np.arange(RADIX)[:, None]
    freq = 4 * np.arange(outer) + 1
    phase = freq[None, :, None] * token[:, None, :] % (4 * sequence)
    angle = 2.0 * np.pi * phase / (4 * sequence)
    forward = np.concatenate([np.cos(angle), -np.sin(angle)], axis=1)
    high, low = host_split(forward)
    twice = np.concatenate([high, high], axis=2)
    inverse = forward.transpose(0, 2, 1) / sequence
    inverse_high, inverse_low = host_split(inverse)
    inverse_pair = np.concatenate([inverse_high, inverse_low], axis=1)
    bands = np.arange(feature_rows // 2)
    turns = token.reshape(1, -1) * (4 * (bands + 1) ** 2)[:, None] % sequence
    turn_angle = 2.0 * np.pi * turns / sequence
    basis = np.concatenate([np.cos(turn_angle), np.sin(turn_angle)], axis=0)
    group = length // RADIX
    order = np.zeros((length, length))
    for r in range(RADIX):
        for v in range(group):
            order[r * group + v, RADIX * v + r] = 1.0
    return (
        jnp.asarray(twice),
        jnp.asarray(low),
        jnp.asarray(inverse_pair),
        jnp.asarray(basis.astype(np.float32)),
        jnp.asarray(order.astype(BF16)),
    )


def dot(left, right, left_dim=1, right_dim=0, precision=None):
    return lax.dot_general(
        left,
        right,
        (((left_dim,), (right_dim,)), ((), ())),
        precision=precision,
        preferred_element_type=F32,
    )


def add(a, b):
    return (a[0] + b[0], a[1] + b[1])


def sub(a, b):
    return (a[0] - b[0], a[1] - b[1])


def quarter(a, inverse):
    return (-a[1], a[0]) if inverse else (a[1], -a[0])


def eighth(a, inverse):
    if inverse:
        return ((a[0] - a[1]) * ROOT_HALF, (a[0] + a[1]) * ROOT_HALF)
    return ((a[0] + a[1]) * ROOT_HALF, (a[1] - a[0]) * ROOT_HALF)


def four_points(a, b, c, d, inverse):
    even_sum, even_diff = add(a, c), sub(a, c)
    odd_sum, odd_diff = add(b, d), quarter(sub(b, d), inverse)
    return (
        add(even_sum, odd_sum),
        add(even_diff, odd_diff),
        sub(even_sum, odd_sum),
        sub(even_diff, odd_diff),
    )


def eight_points(x, inverse):
    even = four_points(x[0], x[2], x[4], x[6], inverse)
    odd = four_points(x[1], x[3], x[5], x[7], inverse)
    first = eighth(odd[1], inverse)
    turned = (odd[0], first, quarter(odd[2], inverse), quarter(eighth(odd[3], inverse), inverse))
    return [add(e, o) for e, o in zip(even, turned)] + [sub(e, o) for e, o in zip(even, turned)]


def times(a, b):
    return (a[0] * b[0] - a[1] * b[1], a[0] * b[1] + a[1] * b[0])


def times_conj(a, b):
    return (a[0] * b[0] + a[1] * b[1], a[1] * b[0] - a[0] * b[1])


def prepare_kernel(
    fin_ref, fout_ref, decay_ref, basis_ref, twice_ref, low_ref,
    hidden_ref, slope_ref, window_ref, taps_ref, spec_ref, leaf_ref,
):
    outer = window_ref.shape[1]
    sequence = RADIX * outer
    scale = sequence ** (-0.5)
    preact = dot(fin_ref[...], basis_ref[...], 0, 0, PRECISE)
    hidden = jnp.sin(preact)
    hidden_ref[...] = hidden
    slope_ref[...] = jnp.cos(preact)
    row = lax.broadcasted_iota(jnp.int32, (outer, LANES), 0)
    for r in range(RADIX):
        fraction = (RADIX * row + r).astype(F32) / sequence
        window = jnp.exp(-decay_ref[...] * fraction)
        window_ref[r] = window
        mix = dot(hidden[:, r * outer : (r + 1) * outer], fout_ref[...], 0, 0, PRECISE)
        taps = window * mix * scale
        taps_ref[r] = taps
        high, low = split(taps)
        leaf_ref[r] = dot(twice_ref[r], jnp.concatenate([high, low], axis=0)) + dot(low_ref[r], high)
    step = 8

    @pl.loop(0, outer // step)
    def _(chunk):
        at = pl.multiple_of(chunk * step, step)
        real = pl.ds(at, step)
        imag = pl.ds(pl.multiple_of(outer + at, step), step)
        points = eight_points([(leaf_ref[r, real, :], leaf_ref[r, imag, :]) for r in range(RADIX)], False)
        for m in range(RADIX):
            spec_ref[m, real, :] = points[m][0]
            spec_ref[m, imag, :] = points[m][1]


def down(block, first_row):
    return jnp.where(first_row, 0.0, pltpu.roll(block, 1, 0))


def up(block, last_row):
    return jnp.where(last_row, 0.0, pltpu.roll(block, block.shape[0] - 1, 0))


def main_kernel(
    in_ref, kern_ref, skip_ref, hidden_ref, slope_ref, window_ref, taps_ref, spec_ref,
    fout_ref, basis_ref, twice_ref, low_ref, pair_ref, order_ref,
    out_ref, grads_ref, first_ref,
    tok_ref, gate_ref, mixgrad_ref, short_ref, leaf_ref, qhigh_ref, qlow_ref, short_grad_ref, weighted_ref, done_ref,
):
    peers, _, lanes, length = in_ref.shape
    outer = taps_ref.shape[1]
    sequence = RADIX * outer
    group = length // RADIX
    scale = sequence ** (-0.5)
    order = order_ref[...]
    for s in range(peers):
        for a in range(4):
            turned = dot(order, in_ref[s, a], 1, 1)
            for r in range(RADIX):
                tok_ref[a, r, s * group : (s + 1) * group, :] = turned[r * group : (r + 1) * group]
    row = lax.broadcasted_iota(jnp.int32, (outer, LANES), 0)
    first_row = row == 0
    last_row = row == outer - 1
    for i in range(3):
        back = [down(tok_ref[i, RADIX - 2], first_row), down(tok_ref[i, RADIX - 1], first_row)]
        weights = [kern_ref[3 * i + j : 3 * i + j + 1, :] for j in range(3)]
        for r in range(RADIX):
            one = back[1] if r == 0 else tok_ref[i, r - 1]
            two = back[r] if r < 2 else tok_ref[i, r - 2]
            short_ref[i, r] = weights[0] * tok_ref[i, r] + weights[1] * one + weights[2] * two
    for r in range(RADIX):
        gate = short_ref[1, r] * short_ref[2, r]
        mixgrad = tok_ref[3, r] * short_ref[0, r]
        gate_ref[r] = gate
        mixgrad_ref[r] = mixgrad
        high, low = split(jnp.concatenate([gate, mixgrad], axis=1))
        leaf_ref[r] = dot(twice_ref[r], jnp.concatenate([high, low], axis=0)) + dot(low_ref[r], high)
    step = 16

    @pl.loop(0, outer // step)
    def _(chunk):
        at = pl.multiple_of(chunk * step, step)
        real = pl.ds(at, step)
        imag = pl.ds(pl.multiple_of(outer + at, step), step)
        spectra = []
        for lane in (0, LANES):
            span = slice(lane, lane + LANES)
            spectra.append(
                eight_points(
                    [(leaf_ref[r, real, span], leaf_ref[r, imag, span]) for r in range(RADIX)], False
                )
            )
        gates, mixes = spectra
        tap = [(spec_ref[m, real, :], spec_ref[m, imag, :]) for m in range(RADIX)]
        products = (
            [times(gates[m], tap[m]) for m in range(RADIX)],
            [times_conj(mixes[m], tap[m]) for m in range(RADIX)],
            [times_conj(mixes[m], gates[m]) for m in range(RADIX)],
        )
        for n in range(3):
            span = slice(n * LANES, (n + 1) * LANES)
            points = eight_points(products[n], True)
            for r in range(RADIX):
                for rows, part in ((real, points[r][0]), (imag, points[r][1])):
                    high, low = split(part)
                    qhigh_ref[r, rows, span] = high
                    qlow_ref[r, rows, span] = low

    skip = skip_ref[...]
    decay_sum = jnp.zeros((1, LANES), F32)
    skip_sum = jnp.zeros((1, LANES), F32)
    for r in range(RADIX):
        both = dot(pair_ref[r], qhigh_ref[r])
        result = both[:outer] + both[outer:] + dot(pair_ref[r, :outer, :], qlow_ref[r])
        gate = gate_ref[r]
        mixgrad = mixgrad_ref[r]
        mixed = result[:, :LANES] + skip * gate
        grad_gate = result[:, LANES : 2 * LANES] + skip * mixgrad
        grad_taps = result[:, 2 * LANES :]
        done_ref[0, r] = (short_ref[0, r] * mixed).astype(BF16)
        short_grad_ref[0, r] = tok_ref[3, r] * mixed
        short_grad_ref[1, r] = grad_gate * short_ref[2, r]
        short_grad_ref[2, r] = grad_gate * short_ref[1, r]
        weighted_ref[r * outer : (r + 1) * outer, :] = grad_taps * window_ref[r] * scale
        fraction = (RADIX * row + r).astype(F32) / sequence
        decay_sum = decay_sum + jnp.sum(grad_taps * taps_ref[r] * -fraction, axis=0, keepdims=True)
        skip_sum = skip_sum + jnp.sum(mixgrad * gate, axis=0, keepdims=True)
    for i in range(3):
        back = [down(tok_ref[i, RADIX - 2], first_row), down(tok_ref[i, RADIX - 1], first_row)]
        ahead = [up(short_grad_ref[i, 0], last_row), up(short_grad_ref[i, 1], last_row)]
        weights = [kern_ref[3 * i + j : 3 * i + j + 1, :] for j in range(3)]
        sums = [jnp.zeros((1, LANES), F32) for _ in range(3)]
        for r in range(RADIX):
            grad = short_grad_ref[i, r]
            next_one = short_grad_ref[i, r + 1] if r + 1 < RADIX else ahead[0]
            next_two = short_grad_ref[i, r + 2] if r + 2 < RADIX else ahead[r + 2 - RADIX]
            done_ref[1 + i, r] = (weights[0] * grad + weights[1] * next_one + weights[2] * next_two).astype(BF16)
            one = back[1] if r == 0 else tok_ref[i, r - 1]
            two = back[r] if r < 2 else tok_ref[i, r - 2]
            for j, value in enumerate((tok_ref[i, r], one, two)):
                sums[j] = sums[j] + jnp.sum(grad * value, axis=0, keepdims=True)
        for j in range(3):
            grads_ref[3 * i + j : 3 * i + j + 1, :] = sums[j] * scale
    grads_ref[9:10, :] = decay_sum * scale
    grads_ref[10:11, :] = skip_sum * scale
    grads_ref[11:16, :] = jnp.zeros((5, LANES), F32)
    weighted = weighted_ref[...]
    grads_ref[16:, :] = dot(hidden_ref[...], weighted, 1, 0, PRECISE) * scale
    grad_hidden = dot(fout_ref[...], weighted, 1, 1, PRECISE)
    first_ref[...] = dot(basis_ref[...], grad_hidden * slope_ref[...], 1, 1, PRECISE) * scale
    for s in range(peers):
        for a in range(4):
            rows = jnp.concatenate(
                [done_ref[a, r, s * group : (s + 1) * group, :] for r in range(RADIX)], axis=0
            )
            out_ref[s, a] = dot(rows, order, 0, 0).astype(BF16)


def exchange(value, axis, by):
    return lax.ppermute(value, axis, [(i, i ^ by) for i in range(lax.axis_size(axis))])


def blocks_body(
    query_in, key_in, value_in, short_kernel, filter_in, filter_out, filter_decay, skip_gain, grad_out
):
    shards = lax.axis_size("ctx")
    groups = lax.axis_size("chan")
    device = lax.axis_index("ctx")
    channels, length = query_in.shape
    sequence = shards * length
    outer = sequence // RADIX
    mine = channels // shards
    order = filter_out.shape[0]
    features = filter_in.shape[0]
    twice, low, pair, basis, turn = host_tables(sequence, features, length)
    sent = jnp.stack(
        [a.reshape(shards, mine, length) for a in (query_in, key_in, value_in, grad_out)], axis=1
    )
    arrived = lax.all_to_all(sent, "ctx", 0, 0, tiled=True)
    at = device * mine
    kern = lax.dynamic_slice_in_dim(short_kernel.reshape(9, channels), at, mine, 1)
    fout = lax.dynamic_slice_in_dim(filter_out, at, mine, 1)
    decay = lax.dynamic_slice_in_dim(filter_decay[None], at, mine, 1)
    skip = lax.dynamic_slice_in_dim(skip_gain[None], at, mine, 1)
    tokens = jax.ShapeDtypeStruct((RADIX, outer, LANES), F32)
    hidden, slope, window, taps, spec = pl.pallas_call(
        prepare_kernel,
        out_shape=(
            jax.ShapeDtypeStruct((order, sequence), F32),
            jax.ShapeDtypeStruct((order, sequence), F32),
            tokens,
            tokens,
            jax.ShapeDtypeStruct((RADIX, 2 * outer, LANES), F32),
        ),
        scratch_shapes=[pltpu.VMEM((RADIX, 2 * outer, LANES), F32)],
        compiler_params=pltpu.CompilerParams(vmem_limit_bytes=40 << 20),
        name="prepare",
    )(filter_in, fout, decay, basis, twice, low)
    results, grads, first = pl.pallas_call(
        main_kernel,
        out_shape=(
            jax.ShapeDtypeStruct(arrived.shape, BF16),
            jax.ShapeDtypeStruct((16 + order, LANES), F32),
            jax.ShapeDtypeStruct((features, order), F32),
        ),
        scratch_shapes=[
            pltpu.VMEM((4, RADIX, outer, LANES), F32),
            pltpu.VMEM((RADIX, outer, LANES), F32),
            pltpu.VMEM((RADIX, outer, LANES), F32),
            pltpu.VMEM((3, RADIX, outer, LANES), F32),
            pltpu.VMEM((RADIX, 2 * outer, 2 * LANES), F32),
            pltpu.VMEM((RADIX, 2 * outer, 3 * LANES), BF16),
            pltpu.VMEM((RADIX, 2 * outer, 3 * LANES), BF16),
            pltpu.VMEM((3, RADIX, outer, LANES), F32),
            pltpu.VMEM((sequence, LANES), F32),
            pltpu.VMEM((4, RADIX, outer, LANES), BF16),
        ],
        compiler_params=pltpu.CompilerParams(vmem_limit_bytes=56 << 20),
        name="main",
    )(arrived, kern, skip, hidden, slope, window, taps, spec, fout, basis, twice, low, pair, turn)
    returned = lax.all_to_all(results, "ctx", 0, 0, tiled=True)
    total = first.reshape(-1, LANES)
    by = 1
    while by < groups:
        total = total + exchange(total, "chan", by)
        by *= 2
    gathered = grads[None]
    by = shards // 2
    while by:
        packed = jnp.concatenate([gathered.reshape(-1, LANES), total], axis=0)
        other = exchange(packed, "ctx", by)
        gathered = jnp.concatenate(
            [gathered, other[: -total.shape[0]].reshape(gathered.shape)], axis=0
        )
        total = total + other[-total.shape[0] :]
        by //= 2
    place = jnp.zeros((shards,), jnp.int32)
    index = jnp.arange(shards, dtype=jnp.int32) ^ device
    by, weight = shards // 2, 1
    while by:
        place = place + jnp.where(index & by, weight, 0)
        by, weight = by // 2, weight * 2
    gathered = gathered[place].transpose(1, 0, 2).reshape(-1, channels)
    outs = [returned[:, a].reshape(channels, length) for a in range(4)]
    return (
        *outs,
        gathered[:9].reshape(3, 3, channels),
        total.reshape(features, order),
        gathered[16:],
        gathered[9],
        gathered[10],
    )


def body(*args):
    channels, length = args[0].shape
    shards = lax.axis_size("ctx")
    whole = channels == shards * LANES and length == LANES and shards * length == RADIX * LANES
    return blocks_body(*args) if whole else spread_body(*args)


def solution(mesh):
    placed = (
        P("chan", "ctx"),
        P("chan", "ctx"),
        P("chan", "ctx"),
        P(None, None, "chan"),
        P(),
        P(None, "chan"),
        P("chan"),
        P("chan"),
        P("chan", "ctx"),
    )
    return jax.shard_map(
        body,
        mesh=mesh,
        in_specs=placed,
        out_specs=(
            P("chan", "ctx"),
            P("chan", "ctx"),
            P("chan", "ctx"),
            P("chan", "ctx"),
            P(None, None, "chan"),
            P(),
            P(None, "chan"),
            P("chan"),
            P("chan"),
        ),
        check_vma=False,
    )
```
